32 devices in a mesh: layer: 2 (over core), row: 1, col: 16 (over z, y, x).
Axes of the slice: x: 2, y: 2, z: 4, core: 2. Of those that a mesh axis runs over, the one named last changes fastest.
Arguments:
- x_blocks: bfloat16 [1, 16, 32, 128, 128], P('row', 'col', 'layer'), may hold values from -0.5 to 0.5
- h_blocks: bfloat16 [1, 16, 32, 128, 128], P('row', 'col', 'layer'), may hold values from -1.5 to 1.5
- a_src: int32 [1, 16, 2, 128, 8], P('row', 'col', 'layer'), may hold values from 0 to 15, all different within a row; in each aligned block of 128 rows (0 to 127, 128 to 255, ..., all dimensions but the last counted through in order) at most 96 rows name the same one
- a_off: int32 [1, 16, 2, 128, 8], P('row', 'col', 'layer'), may hold values from 0 to 15
- b_slot: int32 [1, 16, 2, 128, 8], P('row', 'col', 'layer'), may hold values from 0 to 15
Outputs:
- product_blocks: bfloat16 [1, 16, 128, 128, 128], P('row', 'col', 'layer')
The draws below stay inside these ranges and needn't reach their ends.
Inputs may be any that keep to these rules, and one draw needn't show every extreme that they name: `a_src`: the 8 sources of one product block are different; among the rows of one device (one owner and group) no column owner is named by more than 96 contributions, a bound that some block reaches. `b_slot`: index into the column panel of 16 blocks.
All inputs are finite; a program needn't handle non-finite values.
Results may differ from the reference program's by a relative error of at most 0.0051.
Values may be sent and summed in bfloat16 or wider, within the bound.
A program may use at most 192 MiB of HBM per device.

```python
import math
import jax
import jax.numpy as jnp
import numpy as np
from jax import lax

BS = 128
NBD = 16
KT = 16
KL = 8
NPO = 128
CAP = 96
N_LAYER = 2
N_ROW = 1
N_COL = 16


def set_ends(entries, key, low, high):
    longest = entries.shape.index(max(entries.shape))
    spots = []
    for shift in (0, 1):
        where = [jax.random.randint(jax.random.fold_in(key, axis), (), 0, length) for axis, length in enumerate(entries.shape)]
        where[longest] = (where[longest] + shift) % entries.shape[longest]
        spots.append(tuple(where))
    return entries.at[spots[0]].set(low).at[spots[1]].set(high)


def level_of(stream_key, shape, cuts, least, high):
    def one(axis_at, parts):
        steps = jax.random.uniform(jax.random.fold_in(jax.random.fold_in(stream_key, 6), axis_at), (parts,), jnp.float32, least / len(cuts), high / len(cuts))
        return jnp.repeat(jnp.exp(steps), shape[axis_at] // parts).reshape((-1,) + (1,) * (len(shape) - axis_at - 1))

    gain = one(*cuts[0])
    for cut in cuts[1:]:
        gain = gain * one(*cut)
    return gain


def routed_block(rng, own, number, rows, count, top, limit, lean):
    order = jax.random.permutation(rng, count)
    crowded, usual = shares(count, rows * top, limit, lean, True), shares(count, rows * top, limit, lean, False)
    places = jnp.arange(count)

    def named(tallies, turn):
        used = int((tallies > 0).sum())
        fixed = max(1, used // 4)
        passed = fixed + (places - fixed + turn * (used - fixed)) % max(1, count - fixed)
        return jnp.zeros((count,), jnp.int32).at[order[jnp.where(places < fixed, places, passed)]].set(jnp.asarray(tallies, jnp.int32))

    tallies = jnp.where(number % 4 == 0, named(crowded, number // 4), named(usual, number - number // 4 - 1))
    mixed = jax.random.permutation(jax.random.fold_in(own, 3), count)
    donor, receiver = mixed[0:count // 2 * 2:2], mixed[1:count // 2 * 2:2]
    room = jnp.minimum(tallies[donor] - 1, limit - tallies[receiver]) // 2
    room = jnp.where((donor == order[0]) | (receiver == order[0]) | (tallies[receiver] == 0), 0, jnp.maximum(room, 0))
    passed = jax.random.randint(jax.random.fold_in(own, 4), (count // 2,), 0, 1 << 20) % (room + 1)
    tallies = tallies.at[donor].add(-passed).at[receiver].add(passed)
    labels = jnp.searchsorted(jnp.cumsum(tallies), jnp.arange(rows * top), side="right").astype(jnp.int32)
    table = labels.reshape(top, rows).T
    table = table[jax.random.permutation(jax.random.fold_in(own, 1), rows)]
    turn = jax.random.randint(jax.random.fold_in(own, 2), (rows, 1), 0, top)
    return jnp.take_along_axis(table, (jnp.arange(top)[None, :] + turn) % top, axis=1)


def shares(count, total, bound, slope, full):
    portions = [(1 << 20) // math.isqrt(standing ** slope) + 1 for standing in range(1, count + 1)]
    largest = bound if full else min(bound, max(-(-total // count), total * portions[0] // sum(portions)))
    least = 1 if total - largest >= count - 1 else 0
    holding, rest = [largest] + [least] * (count - 1), total - largest - least * (count - 1)
    while rest > 0:
        free = [i for i in range(1, count) if holding[i] < largest] or [i for i in range(1, count) if holding[i] < bound]
        whole, left = sum([portions[i] for i in free]), rest
        for i in free:
            more = min(bound - holding[i], max(1, left * portions[i] // whole), rest)
            holding[i] = holding[i] + more
            rest = rest - more
    return np.array(holding)


def normal_values(key, dims, scale, limit, split=(), kind=jnp.bfloat16):
    factor_of = level_of(key, dims, split, -0.22, 0.18) if split else 1.0
    values = jax.random.normal(key, dims, jnp.float32) * scale * factor_of
    return jnp.minimum(jnp.maximum(values, -limit), limit).astype(kind)


def setup_inputs(seed: int = 0) -> dict:
    key_of = jax.random.split(jax.random.key(seed), 6)
    x_blocks = normal_values(key_of[0], (N_ROW, N_COL, N_LAYER * NBD, BS, BS), BS ** -0.5, 0.5, ((1, 16), (2, 2)))
    h_blocks = normal_values(key_of[1], (N_ROW, N_COL, N_LAYER * NBD, BS, BS), KT ** -0.5, 1.5, ((1, 16), (2, 2)))
    a_src_keys = jax.random.split(jax.random.fold_in(key_of[2], 1), N_ROW * N_COL * N_LAYER * NPO // NPO)
    a_src_turns = jax.random.permutation(jax.random.fold_in(key_of[2], 3), N_ROW * N_COL * N_LAYER * NPO // NPO)
    a_src = jax.vmap(lambda own, number: routed_block(jax.random.fold_in(key_of[2], 2), own, number, NPO, N_COL, KL, CAP, 1))(a_src_keys, a_src_turns).reshape((N_ROW, N_COL, N_LAYER, NPO, KL))
    a_off = set_ends(jax.random.randint(key_of[3], (N_ROW, N_COL, N_LAYER, NPO, KL), 0, NBD), jax.random.fold_in(key_of[3], 1), 0, NBD - 1).astype(jnp.int32)
    b_slot = set_ends(jax.random.randint(key_of[4], (N_ROW, N_COL, N_LAYER, NPO, KL), 0, N_ROW * NBD), jax.random.fold_in(key_of[4], 1), 0, (N_ROW * NBD) - 1).astype(jnp.int32)
    return dict(x_blocks=x_blocks, h_blocks=h_blocks, a_src=a_src, a_off=a_off, b_slot=b_slot)


def reference(x_blocks, h_blocks, a_src, a_off, b_slot):
    def one_owner(index):
        rowid = index // N_COL
        colid = index % N_COL
        x_row = lax.dynamic_index_in_dim(x_blocks, rowid, 0, keepdims=False)
        h_col = lax.dynamic_index_in_dim(h_blocks, colid, 1, keepdims=False)
        src_own = lax.dynamic_index_in_dim(lax.dynamic_index_in_dim(a_src, rowid, 0, keepdims=False), colid, 0, keepdims=False)
        off_own = lax.dynamic_index_in_dim(lax.dynamic_index_in_dim(a_off, rowid, 0, keepdims=False), colid, 0, keepdims=False)
        b_own = lax.dynamic_index_in_dim(lax.dynamic_index_in_dim(b_slot, rowid, 0, keepdims=False), colid, 0, keepdims=False)
        total = jnp.zeros((NPO, BS, BS), jnp.float32)
        for group in range(N_LAYER):
            row_panel = x_row[:, group * NBD:(group + 1) * NBD].reshape(N_COL * NBD, BS, BS)
            col_panel = h_col[:, group * NBD:(group + 1) * NBD].reshape(N_ROW * NBD, BS, BS)
            partial_value = jnp.zeros((NPO, BS, BS), jnp.float32)
            for term in range(KL):
                where_left = (src_own[group, :, term] * NBD + off_own[group, :, term]).astype(jnp.int32)
                left = row_panel[where_left].astype(jnp.float32)
                right = col_panel[b_own[group, :, term]].astype(jnp.float32)
                partial_value = partial_value + jnp.einsum("pij,pjk->pik", left, right)
            rounded = lax.optimization_barrier(partial_value.astype(jnp.bfloat16))
            total = total + rounded.astype(jnp.float32)
        return total.astype(jnp.bfloat16)

    result = lax.map(one_owner, jnp.arange(N_ROW * N_COL, dtype=jnp.int32))
    return result.reshape(N_ROW, N_COL, NPO, BS, BS)
```

```python
import functools

import jax
import jax.numpy as jnp
from jax import lax
from jax.experimental import pallas as pl
from jax.experimental.pallas import tpu as pltpu
from jax.sharding import PartitionSpec as P


def product_kernel(rows, keep, src_ref, off_ref, slot_ref, panel_ref, h_ref, out_ref):
    per_src = panel_ref.shape[1]
    terms = src_ref.shape[1]
    layer = lax.axis_index("layer")
    start = (layer if keep else 1 - layer) * rows

    @pl.loop(0, rows, unroll=4)
    def _(p):
        row = start + p
        left = [panel_ref[src_ref[row, k], off_ref[row, k]] for k in range(terms)]
        right = [h_ref[slot_ref[row, k]] for k in range(terms)]
        out_ref[p] = jnp.dot(
            jnp.concatenate(left, axis=1),
            jnp.concatenate(right, axis=0),
            preferred_element_type=jnp.float32,
        ).astype(out_ref.dtype)


def products(keep, src, off, slot, panel, h):
    rows = src.shape[0] // 2
    bs = h.shape[-1]
    smem = pl.BlockSpec(memory_space=pltpu.SMEM)
    vmem = pl.BlockSpec(memory_space=pltpu.VMEM)
    return pl.pallas_call(
        functools.partial(product_kernel, rows, keep),
        out_shape=jax.ShapeDtypeStruct((rows, bs, bs), jnp.bfloat16),
        in_specs=[smem, smem, smem, vmem, vmem],
        out_specs=vmem,
        compiler_params=pltpu.CompilerParams(vmem_limit_bytes=40 << 20),
        cost_estimate=pl.CostEstimate(
            flops=2 * rows * src.shape[1] * bs**3,
            bytes_accessed=panel.size * 2 + h.size * 2 + rows * bs * bs * 2,
            transcendentals=0,
        ),
    )(src, off, slot, panel, h)


def on_device(x_blocks, h_blocks, a_src, a_off, b_slot):
    x_local = x_blocks[0, 0]
    h = lax.all_gather(h_blocks[0, 0], "row", axis=0, tiled=True)
    panel = lax.all_gather(x_local, "col", axis=0, tiled=False)
    lists = (a_src[0, 0, 0], a_off[0, 0, 0], b_slot[0, 0, 0])
    theirs = products(False, *lists, panel, h)
    arrived = lax.ppermute(theirs, "layer", [(0, 1), (1, 0)])
    mine = products(True, *lists, panel, h)
    total = mine.astype(jnp.float32) + arrived.astype(jnp.float32)
    return total.astype(jnp.bfloat16)[None, None]


def solution(mesh):
    placed = P("row", "col", "layer", None, None)
    return jax.shard_map(
        on_device,
        mesh=mesh,
        in_specs=(placed,) * 5,
        out_specs=placed,
        check_vma=False,
    )
```

```python
import functools
import itertools

import jax
import jax.numpy as jnp
from jax import lax
from jax.experimental import pallas as pl
from jax.experimental.pallas import tpu as pltpu
from jax.sharding import PartitionSpec as P

CHUNKS = 8
ORDERS = (((0, 2, 1), 4), ((1, 2, 0), 4), ((2, 0, 1), 4), ((2, 1, 0), 4))


def line_sizes(cols):
    x = 2
    z = 4 if cols % 8 == 0 else 1
    return (x, cols // (x * z), z)


def shares(blocks):
    found, low = [], 0
    for order, part in ORDERS:
        high = low + max(1, blocks * part // 16)
        found.append((order, low, high))
        low = high
    return tuple(found)


def steps_of(size):
    found = [0]
    for far in range(1, size):
        found += [far] if size == 2 else [far, -far]
    return found


class Spread:
    def __init__(self, x_ref, panel, send_sem, recv_sem):
        self.x_ref, self.panel, self.send_sem, self.recv_sem = x_ref, panel, send_sem, recv_sem
        self.sizes = line_sizes(panel.shape[0])
        self.parts = shares(panel.shape[1])
        self.me = lax.axis_index("col")
        rest, self.at = self.me, []
        for size in self.sizes:
            self.at.append(lax.rem(rest, size))
            rest = lax.div(rest, size)

    def index(self, at):
        return (at[2] * self.sizes[1] + at[1]) * self.sizes[0] + at[0]

    def source(self, rel):
        at, ok = [], None
        for here, step, size in zip(self.at, rel, self.sizes):
            if size == 2:
                at.append(lax.rem(here + step, 2))
            else:
                at.append(here + step)
                if step:
                    inside = here + step < size if step > 0 else here + step >= 0
                    ok = inside if ok is None else jnp.logical_and(ok, inside)
        return at, ok

    def ways(self, dim):
        size = self.sizes[dim]
        if size == 1:
            return []
        stride = 1
        for other in self.sizes[:dim]:
            stride *= other
        here = self.at[dim]
        if size == 2:
            return [(2 * dim, self.me + (1 - 2 * here) * stride, None, 0)]
        return [
            (2 * dim, self.me + stride, here + 1 < size, 1),
            (2 * dim + 1, self.me - stride, here >= 1, -1),
        ]

    def greet(self):
        barrier = pltpu.get_barrier_semaphore()
        count = 0
        for dim in range(3):
            for _, other, ok, _ in self.ways(dim):
                def hail(other=other):
                    pl.semaphore_signal(
                        barrier, inc=1, device_id={"col": other}, device_id_type=pl.DeviceIdType.MESH
                    )
                if ok is None:
                    hail()
                    count = count + 1
                else:
                    pl.when(ok)(hail)
                    count = count + ok.astype(jnp.int32)
        return barrier, count

    def copy(self, part, own, src, slot, other):
        _, low, high = self.parts[part]
        blocks = pl.ds(low, high - low)
        return pltpu.make_async_remote_copy(
            src_ref=self.x_ref.at[blocks] if own else self.panel.at[src, blocks],
            dst_ref=self.panel.at[src, blocks],
            send_sem=self.send_sem.at[part, src, slot],
            recv_sem=self.recv_sem.at[part, src],
            device_id={"col": other},
            device_id_type=pl.DeviceIdType.MESH,
        )

    def onward(self, part, rel):
        order = self.parts[part][0]
        moved = [place for place in range(3) if rel[order[place]]]
        last = moved[-1] if moved else -1
        found = []
        if moved:
            dim = order[last]
            if self.sizes[dim] > 2:
                found += [way for way in self.ways(dim) if way[3] * rel[dim] < 0]
        for place in range(last + 1, 3):
            found += self.ways(order[place])
        return found

    def events(self):
        rels = itertools.product(*(steps_of(size) for size in self.sizes))
        found = [
            (part, rel)
            for rel in rels
            for part in range(len(self.parts))
        ]
        def when(event):
            part, rel = event
            order = self.parts[part][0]
            hops = sum(abs(step) for step in rel)
            final = rel[order[2]] != 0 and self.sizes[order[2]] == 2
            return (final, hops, abs(rel[2]), part)
        return sorted(found, key=when)

    def visit(self, part, rel, act):
        at, ok = self.source(rel)
        src = self.index(at)
        def body():
            act(src)
        if ok is None:
            body()
        else:
            pl.when(ok)(body)

    def start_onward(self, part, rel, src):
        own = not any(rel)
        for slot, other, ok, _ in self.onward(part, rel):
            send = self.copy(part, own, src, slot, other).start
            if ok is None:
                send()
            else:
                pl.when(ok)(send)

    def wait_sent(self, part, rel, src):
        own = not any(rel)
        for slot, other, ok, _ in self.onward(part, rel):
            wait = self.copy(part, own, src, slot, other).wait_send
            if ok is None:
                wait()
            else:
                pl.when(ok)(wait)

    def run(self):
        for part, rel in self.events():
            def act(src, part=part, rel=rel):
                if any(rel):
                    self.copy(part, False, src, 0, self.ways(0)[0][1]).wait_recv()
                self.start_onward(part, rel, src)
            self.visit(part, rel, act)

    def finish(self):
        for part, rel in self.events():
            self.visit(part, rel, lambda src, part=part, rel=rel: self.wait_sent(part, rel, src))


def kernel(
    code_ref, x_ref, h_ref, out_ref,
    panel, theirs, arrived, own_sem, send_sem, recv_sem, swap_send, swap_recv,
):
    layer = lax.axis_index("layer")
    rows, terms = code_ref.shape
    keep = rows // 2
    slots = h_ref.shape[0]
    per_src = x_ref.shape[0]
    spread = Spread(x_ref, panel, send_sem, recv_sem)
    barrier, count = spread.greet()
    pl.semaphore_signal(
        barrier, inc=1, device_id={"layer": 1 - layer}, device_id_type=pl.DeviceIdType.MESH
    )
    local = pltpu.make_async_copy(x_ref, panel.at[spread.me], own_sem)
    local.start()
    pl.semaphore_wait(barrier, count + 1)
    spread.run()
    local.wait()

    def product(row):
        left, right = [], []
        for k in range(terms):
            code = code_ref[row, k]
            block = lax.div(code, slots)
            left.append(panel[lax.div(block, per_src), lax.rem(block, per_src)])
            right.append(h_ref[lax.rem(code, slots)])
        return jnp.dot(
            jnp.concatenate(left, axis=1),
            jnp.concatenate(right, axis=0),
            preferred_element_type=jnp.float32,
        ).astype(jnp.bfloat16)

    size = keep // CHUNKS

    def swap(chunk):
        part = pl.ds(chunk * size, size)
        return pltpu.make_async_remote_copy(
            src_ref=theirs.at[part],
            dst_ref=arrived.at[part],
            send_sem=swap_send.at[chunk],
            recv_sem=swap_recv.at[chunk],
            device_id={"layer": 1 - layer},
            device_id_type=pl.DeviceIdType.MESH,
        )

    @pl.loop(0, CHUNKS)
    def _(chunk):
        @pl.loop(0, size, unroll=4)
        def _(i):
            p = chunk * size + i
            theirs[p] = product((1 - layer) * keep + p)
        swap(chunk).start()

    @pl.loop(0, CHUNKS)
    def _(chunk):
        swap(chunk).wait_recv()

        @pl.loop(0, size, unroll=4)
        def _(i):
            p = chunk * size + i
            total = product(layer * keep + p).astype(jnp.float32) + arrived[p].astype(jnp.float32)
            out_ref[p] = total.astype(out_ref.dtype)

    spread.finish()

    @pl.loop(0, CHUNKS)
    def _(chunk):
        swap(chunk).wait_send()


def on_device(cols, x_blocks, h_blocks, a_src, a_off, b_slot):
    x_local = x_blocks[0, 0]
    h = lax.all_gather(h_blocks[0, 0], "row", axis=0, tiled=True)
    per_src, bs = x_local.shape[0], x_local.shape[1]
    rows = a_src.shape[3]
    slots = h.shape[0]
    code = ((a_src * per_src + a_off) * slots + b_slot)[0, 0, 0]
    parts = len(shares(per_src))
    vmem = pl.BlockSpec(memory_space=pltpu.VMEM)
    out = pl.pallas_call(
        kernel,
        out_shape=jax.ShapeDtypeStruct((rows // 2, bs, bs), jnp.bfloat16),
        in_specs=[pl.BlockSpec(memory_space=pltpu.SMEM), vmem, vmem],
        out_specs=vmem,
        scratch_shapes=[
            pltpu.VMEM((cols, per_src, bs, bs), jnp.bfloat16),
            pltpu.VMEM((rows // 2, bs, bs), jnp.bfloat16),
            pltpu.VMEM((rows // 2, bs, bs), jnp.bfloat16),
            pltpu.SemaphoreType.DMA,
            pltpu.SemaphoreType.DMA((parts, cols, 6)),
            pltpu.SemaphoreType.DMA((parts, cols)),
            pltpu.SemaphoreType.DMA((CHUNKS,)),
            pltpu.SemaphoreType.DMA((CHUNKS,)),
        ],
        compiler_params=pltpu.CompilerParams(
            collective_id=0, has_side_effects=True, vmem_limit_bytes=48 << 20
        ),
    )(code, x_local, h)
    return out[None, None]


def solution(mesh):
    placed = P("row", "col", "layer", None, None)
    return jax.shard_map(
        functools.partial(on_device, mesh.shape["col"]),
        mesh=mesh,
        in_specs=(placed,) * 5,
        out_specs=placed,
        check_vma=False,
    )
```

```python
import functools
import itertools

import jax
import jax.numpy as jnp
from jax import lax
from jax.experimental import pallas as pl
from jax.experimental.pallas import tpu as pltpu
from jax.sharding import PartitionSpec as P

CHUNKS = 8
STAGES = (8,)
ORDERS = (((0, 2, 1), 4), ((1, 2, 0), 4), ((2, 0, 1), 4), ((2, 1, 0), 4))


def line_sizes(cols):
    x = 2
    z = 4 if cols % 8 == 0 else 1
    return (x, cols // (x * z), z)


def shares(blocks):
    found, low = [], 0
    for order, part in ORDERS:
        high = low + max(1, blocks * part // 16)
        found.append((order, low, high))
        low = high
    return tuple(found)


def steps_of(size):
    found = [0]
    for far in range(1, size):
        found += [far] if size == 2 else [far, -far]
    return found


def guarded(room, act):
    if room:
        pl.when(functools.reduce(jnp.minimum, room) >= 0)(act)
    else:
        act()


class Spread:
    def __init__(self, x_ref, panel, send_sem, recv_sem):
        self.x_ref, self.panel, self.send_sem, self.recv_sem = x_ref, panel, send_sem, recv_sem
        self.per_src = x_ref.shape[0]
        self.sizes = line_sizes(panel.shape[0] // self.per_src)
        self.parts = shares(self.per_src)
        self.me = lax.axis_index("col")
        rest, self.at = self.me, []
        for size in self.sizes:
            self.at.append(lax.rem(rest, size))
            rest = lax.div(rest, size)

    def index(self, at):
        return (at[2] * self.sizes[1] + at[1]) * self.sizes[0] + at[0]

    def source(self, rel):
        at, room = [], []
        for here, step, size in zip(self.at, rel, self.sizes):
            if size == 2:
                at.append(lax.rem(here + step, 2))
            else:
                at.append(here + step)
                if step:
                    room.append(size - 1 - here - step if step > 0 else here + step)
        return at, room

    def ways(self, dim):
        size = self.sizes[dim]
        if size == 1:
            return []
        stride = 1
        for other in self.sizes[:dim]:
            stride *= other
        here = self.at[dim]
        if size == 2:
            return [(2 * dim, self.me + (1 - 2 * here) * stride, [], 0)]
        return [
            (2 * dim, self.me + stride, [size - 2 - here], 1),
            (2 * dim + 1, self.me - stride, [here - 1], -1),
        ]

    def greet(self):
        barrier = pltpu.get_barrier_semaphore()
        count = 0
        for dim in range(3):
            for _, other, room, _ in self.ways(dim):
                def hail(other=other):
                    pl.semaphore_signal(
                        barrier, inc=1, device_id={"col": other}, device_id_type=pl.DeviceIdType.MESH
                    )
                guarded(room, hail)
                count = count + (jnp.where(room[0] >= 0, 1, 0) if room else 1)
        return barrier, count

    def copy(self, part, own, src, slot, other):
        _, low, high = self.parts[part]
        blocks = pl.ds(low, high - low)
        landing = pl.ds(src * self.per_src + low, high - low)
        return pltpu.make_async_remote_copy(
            src_ref=self.x_ref.at[blocks] if own else self.panel.at[landing],
            dst_ref=self.panel.at[landing],
            send_sem=self.send_sem.at[part, src, slot],
            recv_sem=self.recv_sem.at[part, src],
            device_id={"col": other},
            device_id_type=pl.DeviceIdType.MESH,
        )

    def onward(self, part, rel):
        order = self.parts[part][0]
        moved = [place for place in range(3) if rel[order[place]]]
        last = moved[-1] if moved else -1
        found = []
        if moved:
            dim = order[last]
            if self.sizes[dim] > 2:
                found += [way for way in self.ways(dim) if way[3] * rel[dim] < 0]
        for place in range(last + 1, 3):
            found += self.ways(order[place])
        return found

    def is_final(self, part, far):
        last = self.parts[part][0][2]
        return self.sizes[last] == 2 and far[last] != 0

    def events(self):
        rels = itertools.product(*(steps_of(size) for size in self.sizes))
        found = [(part, rel) for rel in rels for part in range(len(self.parts))]
        return sorted(found, key=lambda e: (sum(map(abs, e[1])), abs(e[1][2]), e[0]))

    def ranked(self):
        nears = itertools.product(*(range(size) for size in self.sizes))
        parts = range(len(self.parts))
        found = []
        for near in sorted(nears, key=lambda n: (sum(self.is_final(q, n) for q in parts), sum(n), n)):
            at = []
            for here, rank, size in zip(self.at, near, self.sizes):
                if size == 2:
                    at.append(lax.rem(here + rank, 2))
                else:
                    place = 0
                    for h in range(size):
                        nearest = sorted(range(size), key=lambda o: (abs(o - h), o))
                        place = place + jnp.where(here == h, nearest[rank], 0)
                    at.append(place)
            found.append((near, self.index(at)))
        return found

    def wait_finals(self, near, src):
        for part in range(len(self.parts)):
            if self.is_final(part, near):
                self.copy(part, False, src, 0, self.ways(0)[0][1]).wait_recv()

    def start_onward(self, part, rel, src):
        own = not any(rel)
        for slot, other, room, _ in self.onward(part, rel):
            guarded(room, self.copy(part, own, src, slot, other).start)

    def run(self):
        for part, rel in self.events():
            if self.is_final(part, rel) or not any(rel):
                continue
            at, room = self.source(rel)
            src = self.index(at)

            def act(src=src, part=part, rel=rel):
                self.copy(part, False, src, 0, self.ways(0)[0][1]).wait_recv()
                self.start_onward(part, rel, src)

            guarded(room, act)

    def finish(self):
        for part, rel in self.events():
            at, room = self.source(rel)
            src = self.index(at)
            for slot, other, more, _ in self.onward(part, rel):
                guarded(room + more, self.copy(part, not any(rel), src, slot, other).wait_send)


def sort_terms(keys, others):
    count = len(keys)
    lists = [list(keys)] + [list(other) for other in others]

    def exchange(i, j):
        swap = lists[0][i] > lists[0][j]
        for each in lists:
            low, high = each[i], each[j]
            each[i], each[j] = jnp.where(swap, high, low), jnp.where(swap, low, high)

    p = 1
    while p < count:
        k = p
        while k >= 1:
            for j in range(k % p, count - k, 2 * k):
                for i in range(min(k, count - j - k)):
                    if (i + j) // (2 * p) == (i + j + k) // (2 * p):
                        exchange(i + j, i + j + k)
            k //= 2
        p *= 2
    return lists[1:]


def kernel(
    src_ref, off_ref, slot_ref, x_ref, h_hbm, out_ref,
    panel, ready, total, h_ref, theirs, arrived, lists, index,
    own_sem, h_sem, index_sem, ready_sem, send_sem, recv_sem, swap_send, swap_recv,
):
    layer = lax.axis_index("layer")
    terms, rows = src_ref.shape
    keep = rows // 2
    per_src = x_ref.shape[0]
    cols = panel.shape[0] // per_src
    spread = Spread(x_ref, panel, send_sem, recv_sem)
    barrier, count = spread.greet()
    pl.semaphore_signal(
        barrier, inc=1, device_id={"layer": 1 - layer}, device_id_type=pl.DeviceIdType.MESH
    )
    local = pltpu.make_async_copy(x_ref, panel.at[pl.ds(spread.me * per_src, per_src)], own_sem)
    local.start()
    load_h = pltpu.make_async_copy(h_hbm, h_ref, h_sem)
    load_h.start()
    ranked = spread.ranked()
    pl.semaphore_wait(barrier, count + 1)
    own = (0, 0, 0)
    for part in range(len(spread.parts)):
        spread.start_onward(part, own, spread.me)

    source = src_ref[...]
    rank = jnp.zeros_like(source)
    for place, (_, src) in enumerate(ranked):
        rank = rank + jnp.where(source == src, place, 0)
    block = source * per_src + off_ref[...]
    slot = slot_ref[...]
    pick = lambda v: [v[k : k + 1] for k in range(terms)]
    blocks, slots = sort_terms(pick(rank), (pick(block), pick(slot)))
    for k in range(terms):
        lists[k : k + 1, :] = blocks[k]
        lists[terms + k : terms + k + 1, :] = slots[k]
    to_index = pltpu.make_async_copy(lists, index, index_sem)
    to_index.start()

    local.wait()
    spread.run()
    to_index.wait()
    load_h.wait()

    def product(held, row, first, last):
        left = [held[index[k, row]] for k in range(first, last)]
        right = [h_ref[index[terms + k, row]] for k in range(first, last)]
        return jnp.dot(
            jnp.concatenate(left, axis=1),
            jnp.concatenate(right, axis=0),
            preferred_element_type=jnp.float32,
        )

    first, complete = 0, 0
    for width in STAGES[:-1]:
        last = first + width
        fresh = []
        for near, src in ranked[complete : cols - terms + last]:
            spread.wait_finals(near, src)
            where = pl.ds(src * per_src, per_src)
            copy = pltpu.make_async_copy(panel.at[where], ready.at[where], ready_sem.at[src])
            copy.start()
            fresh.append(copy)
        complete = cols - terms + last
        for copy in fresh:
            copy.wait()

        @pl.loop(0, rows, unroll=4)
        def _(row, first=first, last=last):
            value = product(ready, row, first, last)
            total[row] = value if first == 0 else total[row] + value

        first = last
    for near, src in ranked[complete:]:
        spread.wait_finals(near, src)

    def partial(row):
        value = product(panel, row, first, terms)
        return (total[row] + value if first else value).astype(jnp.bfloat16)

    size = keep // CHUNKS

    def swap(chunk):
        part = pl.ds(chunk * size, size)
        return pltpu.make_async_remote_copy(
            src_ref=theirs.at[part],
            dst_ref=arrived.at[part],
            send_sem=swap_send.at[chunk],
            recv_sem=swap_recv.at[chunk],
            device_id={"layer": 1 - layer},
            device_id_type=pl.DeviceIdType.MESH,
        )

    @pl.loop(0, CHUNKS)
    def _(chunk):
        @pl.loop(0, size, unroll=4)
        def _(i):
            p = chunk * size + i
            theirs[p] = partial((1 - layer) * keep + p)
        swap(chunk).start()

    @pl.loop(0, CHUNKS)
    def _(chunk):
        swap(chunk).wait_recv()

        @pl.loop(0, size, unroll=4)
        def _(i):
            p = chunk * size + i
            both = partial(layer * keep + p).astype(jnp.float32) + arrived[p].astype(jnp.float32)
            out_ref[p] = both.astype(out_ref.dtype)

    spread.finish()

    @pl.loop(0, CHUNKS)
    def _(chunk):
        swap(chunk).wait_send()


def on_device(cols, x_blocks, h_blocks, a_src, a_off, b_slot):
    x_local = x_blocks[0, 0]
    h = lax.all_gather(h_blocks[0, 0], "row", axis=0, tiled=True)
    per_src, bs = x_local.shape[0], x_local.shape[1]
    rows, terms = a_src.shape[3:]
    parts = len(shares(per_src))
    vmem = pl.BlockSpec(memory_space=pltpu.VMEM)
    hbm = pl.BlockSpec(memory_space=pltpu.HBM)
    panel = pltpu.VMEM((cols * per_src, bs, bs), jnp.bfloat16)
    half = pltpu.VMEM((rows // 2, bs, bs), jnp.bfloat16)
    out = pl.pallas_call(
        kernel,
        out_shape=jax.ShapeDtypeStruct((rows // 2, bs, bs), jnp.bfloat16),
        in_specs=[vmem, vmem, vmem, vmem, hbm],
        out_specs=vmem,
        scratch_shapes=[
            panel,
            panel,
            pltpu.VMEM((rows, bs, bs), jnp.float32),
            pltpu.VMEM(h.shape, jnp.bfloat16),
            half,
            half,
            pltpu.VMEM((2 * terms, rows), jnp.int32),
            pltpu.SMEM((2 * terms, rows), jnp.int32),
            pltpu.SemaphoreType.DMA,
            pltpu.SemaphoreType.DMA,
            pltpu.SemaphoreType.DMA,
            pltpu.SemaphoreType.DMA((cols,)),
            pltpu.SemaphoreType.DMA((parts, cols, 6)),
            pltpu.SemaphoreType.DMA((parts, cols)),
            pltpu.SemaphoreType.DMA((CHUNKS,)),
            pltpu.SemaphoreType.DMA((CHUNKS,)),
        ],
        compiler_params=pltpu.CompilerParams(
            collective_id=0, has_side_effects=True, vmem_limit_bytes=56 << 20
        ),
    )(a_src[0, 0, 0].T, a_off[0, 0, 0].T, b_slot[0, 0, 0].T, x_local, h)
    return out[None, None]


def solution(mesh):
    placed = P("row", "col", "layer", None, None)
    return jax.shard_map(
        functools.partial(on_device, mesh.shape["col"]),
        mesh=mesh,
        in_specs=(placed,) * 5,
        out_specs=placed,
        check_vma=False,
    )
```
